32 devices in a mesh: dp: 8 (over z, x), tensor: 4 (over y, core).
Axes of the slice: x: 2, y: 2, z: 4, core: 2. Of those that a mesh axis runs over, the one named last changes fastest.
Arguments:
- tokens: bfloat16 [4096, 768], P(('dp', 'tensor')), may hold values from -6 to 6
- cotangent: float32 [4096, 768], P(('dp', 'tensor')), may hold values from -6 to 6
- ln_gains: float32 [1, 2, 768], P(None, None, ('dp', 'tensor')), may hold values from 0.5 to 1.5
- ln_biases: float32 [1, 2, 768], P(None, None, ('dp', 'tensor')), may hold values from -4 to 4
- out_biases: float32 [1, 2, 768], P(None, None, ('dp', 'tensor')), may hold values from -6 to 6
- w_qkv: bfloat16 [1, 768, 12, 192], P(None, 'dp', 'tensor'), may hold values from -0.21875 to 0.21875
- b_qkv: bfloat16 [1, 12, 192], P(None, 'tensor', 'dp'), may hold values from -6 to 6
- w_out: bfloat16 [1, 12, 64, 768], P(None, 'tensor', None, 'dp'), may hold values from -0.875 to 0.875
- w_in: bfloat16 [1, 768, 3072], P(None, 'dp', 'tensor'), may hold values from -0.21875 to 0.21875
- b_in: bfloat16 [1, 24, 128], P(None, 'tensor', 'dp'), may hold values from -6 to 6
- w_mlp: bfloat16 [1, 3072, 768], P(None, 'tensor', 'dp'), may hold values from -0.109375 to 0.109375
Outputs:
- activations: float32 [4096, 768], P(('dp', 'tensor'))
- input_grad: float32 [4096, 768], P(('dp', 'tensor'))
- grad_ln_gains: float32 [1, 2, 768], P(None, None, ('dp', 'tensor'))
- grad_ln_biases: float32 [1, 2, 768], P(None, None, ('dp', 'tensor'))
- grad_out_biases: float32 [1, 2, 768], P(None, None, ('dp', 'tensor'))
- grad_w_qkv: float32 [1, 768, 12, 192], P(None, 'dp', 'tensor')
- grad_b_qkv: float32 [1, 12, 192], P(None, 'tensor', 'dp')
- grad_w_out: float32 [1, 12, 64, 768], P(None, 'tensor', None, 'dp')
- grad_w_in: float32 [1, 768, 3072], P(None, 'dp', 'tensor')
- grad_b_in: float32 [1, 24, 128], P(None, 'tensor', 'dp')
- grad_w_mlp: float32 [1, 3072, 768], P(None, 'tensor', 'dp')
The draws below stay inside these ranges and needn't reach their ends.
All inputs are finite; a program needn't handle non-finite values.
Results may differ from the reference program's by a relative error of at most 0.04.
The reference program's roundings to bfloat16 on the way count: a program that leaves them out, or rounds other values in their place, can miss the bound.
Values may be sent and summed in bfloat16 or wider, within the bound.
No kernel may reach another device: no remote copies, remote signals or barrier semaphores. Data moves between devices by JAX's collectives and lax.ppermute only.
A program may use at most 64 MiB of HBM per device.

```python
import jax
import jax.numpy as jnp
from jax import lax

D = 768
HEADS = 12
HD = 64
ROT = 16
FF = 3072
LAYERS = 1
SEQ = 512
TOKENS = 4096
N_DP = 8
N_TENSOR = 4


def draw_b_qkv(key, part):
    base = 0.5 * jax.random.normal(jax.random.fold_in(key, 11), (LAYERS, HEADS, 3 * HD), jnp.float32)
    base = jnp.clip(base, -6.0, 6.0)
    return base.astype(jnp.bfloat16)


def shard_levels(own_key, shape, shards, smallest, top_value):
    level, own = 1.0, jax.random.fold_in(own_key, 6)
    for axis_at, blocks in shards:
        draws = jnp.exp(jax.random.uniform(jax.random.fold_in(own, axis_at), (blocks,), jnp.float32, smallest / len(shards), top_value / len(shards)))
        level = level * jnp.repeat(draws, shape[axis_at] // blocks).reshape([-1 if axis == axis_at else 1 for axis in range(len(shape))])
    return level


def gaussian(own_key, dims, deviation, bound, cuts=(), kind=jnp.bfloat16):
    drawn = deviation * jax.random.normal(own_key, dims, jnp.float32)
    if cuts:
        drawn = drawn * shard_levels(own_key, dims, cuts, -0.22, 0.18)
    return jnp.clip(drawn, -bound, bound).astype(kind)


def setup_inputs(seed: int = 0) -> dict:
    arg_keys = jax.random.split(jax.random.key(seed), 12)
    tokens = gaussian(arg_keys[0], (TOKENS, D), 1.0, 6.0, ((0, 32),))
    cotangent = gaussian(arg_keys[1], (TOKENS, D), 1.0, 6.0, ((0, 32),), jnp.float32)
    ln_gains = jnp.clip(1.0 + 0.1 * jax.random.normal(arg_keys[2], (LAYERS, 2, D), jnp.float32), 0.5, 1.5)
    ln_biases = gaussian(arg_keys[3], (LAYERS, 2, D), 0.3, 4.0, ((2, 32),), jnp.float32)
    out_biases = gaussian(arg_keys[4], (LAYERS, 2, D), 0.5, 6.0, ((2, 32),), jnp.float32)
    w_qkv = gaussian(arg_keys[5], (LAYERS, D, HEADS, 3 * HD), D ** -0.5, 0.21875, ((1, 8), (2, 4)))
    b_qkv = draw_b_qkv(jax.random.fold_in(arg_keys[11], 71), 0)
    w_out = gaussian(arg_keys[7], (LAYERS, HEADS, HD, D), (HEADS * HD // 16) ** -0.5, 0.875, ((1, 4), (3, 8)))
    w_in = gaussian(arg_keys[8], (LAYERS, D, FF), D ** -0.5, 0.21875, ((1, 8), (2, 4)))
    b_in = gaussian(arg_keys[9], (LAYERS, FF // 128, 128), 0.5, 6.0, ((1, 4), (2, 8)))
    w_mlp = gaussian(arg_keys[10], (LAYERS, FF, D), FF ** -0.5, 0.109375, ((1, 4), (2, 8)))
    return dict(tokens=tokens, cotangent=cotangent, ln_gains=ln_gains, ln_biases=ln_biases, out_biases=out_biases, w_qkv=w_qkv, b_qkv=b_qkv, w_out=w_out, w_in=w_in, b_in=b_in, w_mlp=w_mlp)


eps = 1e-05

def rounded(value_rows):
    return lax.optimization_barrier(value_rows.astype(jnp.bfloat16)).astype(jnp.float32)

def gelu(value_rows):
    return 0.5 * value_rows * (1.0 + jax.scipy.special.erf(value_rows * 0.7071067811865476))

def gelu_slope(value_rows):
    return 0.5 * (1.0 + jax.scipy.special.erf(value_rows * 0.7071067811865476)) + value_rows * jnp.exp(-0.5 * value_rows * value_rows) * 0.3989422804014327

def rotary_tables(length):
    half = ROT // 2
    freq = 10000.0 ** (-jnp.arange(half, dtype=jnp.float32) * 2.0 / ROT)
    angle = jnp.arange(length, dtype=jnp.float32)[:, None] * freq[None, :]
    return (jnp.cos(angle), jnp.sin(angle))

def rotate(value_rows, cosine, sine, sign):
    half = ROT // 2
    first_layer = value_rows[:, :, :half]
    second_layer = value_rows[:, :, half:ROT]
    cos_b = cosine[:, None, :]
    sin_b = sine[:, None, :] * sign
    return jnp.concatenate([first_layer * cos_b - second_layer * sin_b, second_layer * cos_b + first_layer * sin_b, value_rows[:, :, ROT:]], axis=2)

def norm_statistics(value_rows):
    centre = value_rows - lax.optimization_barrier(jnp.mean(value_rows, axis=-1, keepdims=True))
    inverse_deviation = lax.rsqrt(lax.optimization_barrier(jnp.mean(centre * centre, axis=-1, keepdims=True)) + eps)
    return (centre * inverse_deviation, inverse_deviation)

def norm_backward(norm_gradient, normalized_state, inverse_deviation, norm_gain):
    scaled_rows = norm_gradient * norm_gain
    return inverse_deviation * (scaled_rows - lax.optimization_barrier(jnp.mean(scaled_rows, axis=-1, keepdims=True)) - normalized_state * lax.optimization_barrier(jnp.mean(scaled_rows * normalized_state, axis=-1, keepdims=True)))

def masked_scores(query_blk, key_all, start, block, length):
    scale = HD ** (-0.5)
    score = jnp.einsum('qhd,khd->hqk', query_blk, key_all, precision=lax.Precision.HIGHEST) * scale
    rows = start + jnp.arange(block, dtype=jnp.int32)
    cols = jnp.arange(length, dtype=jnp.int32)
    return jnp.where(cols[None, None, :] <= rows[None, :, None], score, -1e+30)

def attend(query_rows, key, value_rows):
    length, heads = (query_rows.shape[0], query_rows.shape[1])
    block = min(512, length)
    count = length // block
    query_f, key_f, value_f = (query_rows.astype(jnp.float32), key.astype(jnp.float32), value_rows.astype(jnp.float32))

    def one(index):
        start = index * block
        query_blk = lax.dynamic_slice_in_dim(query_f, start, block, 0)
        score = masked_scores(query_blk, key_f, start, block, length)
        top = lax.optimization_barrier(jnp.max(score, axis=-1, keepdims=True))
        expd = jnp.exp(score - top)
        total = lax.optimization_barrier(jnp.sum(expd, axis=-1, keepdims=True))
        prob = rounded(expd / total)
        context_output = jnp.einsum('hqk,khd->qhd', prob, value_f, precision=lax.Precision.HIGHEST)
        return (context_output.astype(jnp.bfloat16), (top + jnp.log(total))[:, :, 0])
    context_output, log_sum_exp = lax.map(one, jnp.arange(count, dtype=jnp.int32))
    return (context_output.reshape(length, heads, HD), log_sum_exp)

def attend_back(query_rows, key, value_rows, context_output, log_sum_exp, d_context):
    length, heads = (query_rows.shape[0], query_rows.shape[1])
    block = min(512, length)
    count = length // block
    scale = HD ** (-0.5)
    query_f, key_f, value_f = (query_rows.astype(jnp.float32), key.astype(jnp.float32), value_rows.astype(jnp.float32))
    d_ctx = d_context.astype(jnp.float32)
    delta = lax.optimization_barrier(jnp.sum(d_ctx * context_output.astype(jnp.float32), axis=-1))

    def one(carry, index):
        d_key, d_value = carry
        start = index * block
        query_blk = lax.dynamic_slice_in_dim(query_f, start, block, 0)
        d_blk = lax.dynamic_slice_in_dim(d_ctx, start, block, 0)
        delta_blk = lax.dynamic_slice_in_dim(delta, start, block, 0)
        score = masked_scores(query_blk, key_f, start, block, length)
        prob = jnp.exp(score - log_sum_exp[index][:, :, None])
        d_value = d_value + jnp.einsum('hqk,qhd->khd', rounded(prob), d_blk, precision=lax.Precision.HIGHEST)
        d_prob = jnp.einsum('qhd,khd->hqk', d_blk, value_f, precision=lax.Precision.HIGHEST)
        d_score = rounded(prob * (d_prob - jnp.transpose(delta_blk)[:, :, None]))
        d_query = jnp.einsum('hqk,khd->qhd', d_score, key_f, precision=lax.Precision.HIGHEST) * scale
        d_key = d_key + jnp.einsum('hqk,qhd->khd', d_score, query_blk, precision=lax.Precision.HIGHEST) * scale
        return ((d_key, d_value), d_query)
    zeros = jnp.zeros((length, heads, HD), jnp.float32)
    (d_key, d_value), d_query = lax.scan(one, (zeros, zeros), jnp.arange(count, dtype=jnp.int32))
    return (d_query.reshape(length, heads, HD), d_key, d_value)

def layer_forward(hidden_state, layer_params, params, cosine, sine):
    norm_gains, norm_shifts, adds, w_qkv, b_qkv, w_out, w_in, b_in, w_mlp = params
    length = hidden_state.shape[0]
    normalized_state, inverse_deviation = norm_statistics(hidden_state)
    first_layer = (normalized_state * norm_gains[layer_params, 0] + norm_shifts[layer_params, 0]).astype(jnp.bfloat16)
    second_layer = (normalized_state * norm_gains[layer_params, 1] + norm_shifts[layer_params, 1]).astype(jnp.bfloat16)
    qkv = jnp.dot(first_layer, w_qkv[layer_params].reshape(D, -1), preferred_element_type=jnp.float32).reshape(length, HEADS, 3 * HD)
    qkv = qkv + b_qkv[layer_params].astype(jnp.float32)
    query_rows = rotate(qkv[:, :, :HD], cosine, sine, 1.0).astype(jnp.bfloat16)
    key = rotate(qkv[:, :, HD:2 * HD], cosine, sine, 1.0).astype(jnp.bfloat16)
    value_rows = qkv[:, :, 2 * HD:].astype(jnp.bfloat16)
    context_output, log_sum_exp = attend(query_rows, key, value_rows)
    preactivation = jnp.dot(second_layer, w_in[layer_params], preferred_element_type=jnp.float32) + b_in[layer_params].reshape(FF).astype(jnp.float32)
    activation_values = gelu(preactivation).astype(jnp.bfloat16)
    grouped_ctx = context_output.astype(jnp.float32).reshape(length, N_TENSOR, HEADS * HD // N_TENSOR)
    grouped_out = w_out[layer_params].astype(jnp.float32).reshape(N_TENSOR, HEADS * HD // N_TENSOR, D)
    grouped_act = activation_values.astype(jnp.float32).reshape(length, N_TENSOR, FF // N_TENSOR)
    grouped_mlp = w_mlp[layer_params].astype(jnp.float32).reshape(N_TENSOR, FF // N_TENSOR, D)
    attn_parts = jnp.einsum('lnk,nkd->nld', grouped_ctx, grouped_out, precision=lax.Precision.HIGHEST)
    mlp_parts = jnp.einsum('lnk,nkd->nld', grouped_act, grouped_mlp, precision=lax.Precision.HIGHEST)
    summed = lax.optimization_barrier(jnp.sum(rounded(attn_parts + mlp_parts), axis=0))
    output_rows = hidden_state + summed + adds[layer_params, 0] + adds[layer_params, 1]
    return (output_rows, (normalized_state, inverse_deviation, first_layer, second_layer, query_rows, key, value_rows, context_output, log_sum_exp, preactivation, activation_values))

def layer_backward(gradient_value, layer_params, params, keep_mask, cosine, sine):
    norm_gains, norm_shifts, adds, w_qkv, b_qkv, w_out, w_in, b_in, w_mlp = params
    normalized_state, inverse_deviation, first_layer, second_layer, query_rows, key, value_rows, context_output, log_sum_exp, preactivation, activation_values = keep_mask
    length = gradient_value.shape[0]
    d_add = lax.optimization_barrier(jnp.sum(gradient_value, axis=0))
    grad_b = gradient_value.astype(jnp.bfloat16)
    d_mlp = jnp.dot(activation_values.T, grad_b, preferred_element_type=jnp.float32)
    d_act = jnp.dot(grad_b, w_mlp[layer_params].T, preferred_element_type=jnp.float32)
    d_pre = d_act * gelu_slope(preactivation)
    d_in_b = lax.optimization_barrier(jnp.sum(d_pre, axis=0))
    d_pre_b = d_pre.astype(jnp.bfloat16)
    d_in = jnp.dot(second_layer.T, d_pre_b, preferred_element_type=jnp.float32)
    second_layer_gradient = jnp.dot(d_pre_b, w_in[layer_params].T, preferred_element_type=jnp.float32)
    flat = context_output.reshape(length, HEADS * HD)
    d_out = jnp.dot(flat.T, grad_b, preferred_element_type=jnp.float32).reshape(HEADS, HD, D)
    d_ctx = jnp.dot(grad_b, w_out[layer_params].reshape(HEADS * HD, D).T, preferred_element_type=jnp.float32)
    d_ctx = d_ctx.astype(jnp.bfloat16).reshape(length, HEADS, HD)
    d_query, d_key, d_value = attend_back(query_rows, key, value_rows, context_output, log_sum_exp, d_ctx)
    d_query = rotate(d_query, cosine, sine, -1.0)
    d_key = rotate(d_key, cosine, sine, -1.0)
    d_qkv = jnp.concatenate([d_query, d_key, d_value], axis=2)
    d_qkv_b = lax.optimization_barrier(jnp.sum(d_qkv, axis=0))
    d_qkv_h = d_qkv.astype(jnp.bfloat16).reshape(length, HEADS * 3 * HD)
    d_qkv_w = jnp.dot(first_layer.T, d_qkv_h, preferred_element_type=jnp.float32).reshape(D, HEADS, 3 * HD)
    first_layer_gradient = jnp.dot(d_qkv_h, w_qkv[layer_params].reshape(D, -1).T, preferred_element_type=jnp.float32)
    gain_gradient = jnp.stack([lax.optimization_barrier(jnp.sum(first_layer_gradient * normalized_state, axis=0)), lax.optimization_barrier(jnp.sum(second_layer_gradient * normalized_state, axis=0))])
    d_shift = jnp.stack([lax.optimization_barrier(jnp.sum(first_layer_gradient, axis=0)), lax.optimization_barrier(jnp.sum(second_layer_gradient, axis=0))])
    d_adds = jnp.stack([d_add, d_add])
    backward_pass = gradient_value + norm_backward(first_layer_gradient, normalized_state, inverse_deviation, norm_gains[layer_params, 0]) + norm_backward(second_layer_gradient, normalized_state, inverse_deviation, norm_gains[layer_params, 1])
    weight_grads = (gain_gradient, d_shift, d_adds, d_qkv_w, d_qkv_b, d_out, d_in, d_in_b.reshape(FF // 128, 128), d_mlp)
    return (backward_pass, weight_grads)

def reference(tokens, cotangent, ln_gains, ln_biases, out_biases, w_qkv, b_qkv, w_out, w_in, b_in, w_mlp):
    params = (ln_gains, ln_biases, out_biases, w_qkv, b_qkv, w_out, w_in, b_in, w_mlp)
    cosine, sine = rotary_tables(SEQ)
    seq_tokens = tokens.reshape(N_DP, SEQ, D)
    seq_cot = cotangent.reshape(N_DP, SEQ, D)

    def one(totals, items):
        inputs, gradient_value = items
        hidden_state = inputs.astype(jnp.float32)
        kept = []
        for layer_params in range(LAYERS):
            hidden_state, keep_mask = layer_forward(hidden_state, layer_params, params, cosine, sine)
            kept.append(keep_mask)
        per_layer = [None] * LAYERS
        for layer_params in reversed(range(LAYERS)):
            gradient_value, per_layer[layer_params] = layer_backward(gradient_value, layer_params, params, kept[layer_params], cosine, sine)
        stacked = tuple((jnp.stack([per_layer[l][m] for l in range(LAYERS)]) for m in range(9)))
        totals = tuple((a + b for a, b in zip(totals, stacked)))
        return (totals, (hidden_state, gradient_value))
    init = (jnp.zeros(ln_gains.shape, jnp.float32), jnp.zeros(ln_gains.shape, jnp.float32), jnp.zeros(ln_gains.shape, jnp.float32), jnp.zeros(w_qkv.shape, jnp.float32), jnp.zeros(b_qkv.shape, jnp.float32), jnp.zeros(w_out.shape, jnp.float32), jnp.zeros(w_in.shape, jnp.float32), jnp.zeros(b_in.shape, jnp.float32), jnp.zeros(w_mlp.shape, jnp.float32))
    totals, (outs, grads) = lax.scan(one, init, (seq_tokens, seq_cot))
    return (outs.reshape(TOKENS, D), grads.reshape(TOKENS, D), totals[0], totals[1], totals[2], totals[3], totals[4], totals[5], totals[6], totals[7], totals[8])
```

```python
import jax
import jax.numpy as jnp
from jax import lax
from jax.sharding import PartitionSpec as P

HD = 64
ROT = 16
EPS = 1e-05
BF = jnp.bfloat16
F32 = jnp.float32


def dot(a, b, ca, cb):
    return lax.dot_general(a, b, (((ca,), (cb,)), ((), ())), preferred_element_type=F32)


def rotary_tables(length):
    half = ROT // 2
    freq = 10000.0 ** (-jnp.arange(half, dtype=F32) * 2.0 / ROT)
    angle = jnp.arange(length, dtype=F32)[:, None] * freq[None, :]
    return jnp.cos(angle), jnp.sin(angle)


def rotate(v, cosine, sine, sign):
    half = ROT // 2
    a, b = v[:, :, :half], v[:, :, half:ROT]
    c, s = cosine[:, None, :], sine[:, None, :] * sign
    return jnp.concatenate([a * c - b * s, b * c + a * s, v[:, :, ROT:]], axis=2)


def pair_swap(value, n):
    return lax.ppermute(value, "dp", [(i, i ^ 1) for i in range(n)])


def outer_exchange(value, n):
    groups = [[inner + 2 * k for k in range(n // 2)] for inner in range(2)]
    return lax.all_to_all(value, "dp", 0, 0, tiled=True, axis_index_groups=groups)


def local(
    tokens, cotangent, ln_gains, ln_biases, out_biases, w_qkv, b_qkv, w_out, w_in, b_in, w_mlp
):
    n_dp, n_t = lax.axis_size("dp"), lax.axis_size("tensor")
    rows, width = tokens.shape
    length = rows * n_t
    n_out = n_dp // 2
    chunk = width // n_dp
    heads = w_out.shape[1]
    qkv_cols = heads * 3 * HD
    inner = lax.axis_index("dp") % 2
    t_index = lax.axis_index("tensor")

    def to_own(v):
        blocks = v.reshape(v.shape[0], n_out, 2, chunk)
        even = blocks[:, :, 0].reshape(v.shape[0], width // 2)
        odd = blocks[:, :, 1].reshape(v.shape[0], width // 2)
        return jnp.concatenate(
            [jnp.where(inner == 0, even, odd), jnp.where(inner == 0, odd, even)], axis=1
        )

    def from_own(v):
        own = v[:, : width // 2].reshape(v.shape[0], n_out, 1, chunk)
        other = v[:, width // 2 :].reshape(v.shape[0], n_out, 1, chunk)
        even, odd = jnp.where(inner == 0, own, other), jnp.where(inner == 0, other, own)
        return jnp.concatenate([even, odd], axis=2).reshape(v.shape[0], width)

    small = jnp.concatenate(
        [
            ln_gains.reshape(-1),
            ln_biases.reshape(-1),
            out_biases.reshape(-1),
            b_qkv.reshape(-1).astype(F32),
            b_in.reshape(-1).astype(F32),
        ]
    )
    n_all = n_dp * n_t
    small_all = lax.all_to_all(
        jnp.broadcast_to(small[None, None], (n_all, 1, small.shape[0])),
        ("dp", "tensor"), 0, 0, tiled=True,
    ).reshape(n_dp, n_t, small.shape[0])
    piece = chunk // n_t
    vec = small_all[:, :, : 6 * piece].reshape(n_dp, n_t, 6, piece)
    vec = to_own(vec.transpose(2, 0, 1, 3).reshape(6, width))
    gains, shifts, adds = vec[0:2], vec[2:4], vec[4:6]
    mine = lax.dynamic_index_in_dim(small_all, t_index, 1, keepdims=False)
    n_bq = b_qkv.size
    bq = mine[:, 6 * piece : 6 * piece + n_bq].reshape(n_dp, heads, -1)
    bq = bq.transpose(1, 0, 2).reshape(qkv_cols)
    bi = mine[:, 6 * piece + n_bq :].reshape(n_dp, b_in.shape[1], -1)
    bi = bi.transpose(1, 0, 2).reshape(-1)

    parts = (
        jnp.concatenate(
            [w_qkv[0].reshape(chunk, qkv_cols), w_out[0].reshape(heads * HD, chunk).T], axis=1
        ),
        w_in[0],
        w_mlp[0].T,
    )

    def fetch(part):
        own = outer_exchange(jnp.broadcast_to(part[None], (n_out,) + part.shape), n_dp)
        return jnp.concatenate([own, pair_swap(own, n_dp)], axis=0).reshape(width, -1)

    w_att, w_in_all, w_mlp_t = (fetch(p) for p in parts)
    w_qkv_all, w_out_t = w_att[:, :qkv_cols], w_att[:, qkv_cols:]

    eb = cotangent.astype(BF)
    both = jnp.concatenate([to_own(tokens), to_own(eb)], axis=1)
    both = lax.all_to_all(
        jnp.broadcast_to(both[None], (n_t,) + both.shape), "tensor", 0, 0, tiled=True
    ).reshape(length, 2 * width)
    x_all, grad_all = both[:, :width].astype(F32), both[:, width:]
    centre = x_all - jnp.mean(x_all, axis=-1, keepdims=True)
    rstd = lax.rsqrt(jnp.mean(centre * centre, axis=-1, keepdims=True) + EPS)
    xhat = centre * rstd
    n_0 = (xhat * gains[0] + shifts[0]).astype(BF)
    n_1 = (xhat * gains[1] + shifts[1]).astype(BF)

    cosine, sine = rotary_tables(length)
    qkv = (dot(n_0, w_qkv_all, 1, 0) + bq).reshape(length, heads, 3 * HD)
    query = rotate(qkv[:, :, :HD], cosine, sine, 1.0).astype(BF)
    key = rotate(qkv[:, :, HD : 2 * HD], cosine, sine, 1.0).astype(BF)
    value = qkv[:, :, 2 * HD :].astype(BF)
    scale = HD ** (-0.5)
    score = jnp.einsum("qhd,khd->hqk", query, key, preferred_element_type=F32) * scale
    index = jnp.arange(length, dtype=jnp.int32)
    score = jnp.where(index[None, None, :] <= index[None, :, None], score, -1e30)
    top = jnp.max(score, axis=-1, keepdims=True)
    expd = jnp.exp(score - top)
    prob = expd / jnp.sum(expd, axis=-1, keepdims=True)
    prob_b = prob.astype(BF)
    context = jnp.einsum("hqk,khd->qhd", prob_b, value, preferred_element_type=F32).astype(BF)
    flat = context.reshape(length, heads * HD)
    d_ctx = dot(grad_all, w_out_t, 1, 0).astype(BF).reshape(length, heads, HD)
    g_out = dot(grad_all, flat, 0, 0)
    delta = jnp.sum(d_ctx.astype(F32) * context.astype(F32), axis=-1)
    d_value = jnp.einsum("hqk,qhd->khd", prob_b, d_ctx, preferred_element_type=F32)
    d_prob = jnp.einsum("qhd,khd->hqk", d_ctx, value, preferred_element_type=F32)
    d_score = (prob * (d_prob - jnp.transpose(delta)[:, :, None])).astype(BF)
    d_query = jnp.einsum("hqk,khd->qhd", d_score, key, preferred_element_type=F32) * scale
    d_key = jnp.einsum("hqk,qhd->khd", d_score, query, preferred_element_type=F32) * scale
    d_qkv = jnp.concatenate(
        [rotate(d_query, cosine, sine, -1.0), rotate(d_key, cosine, sine, -1.0), d_value], axis=2
    )
    g_bq = jnp.sum(d_qkv, axis=0)
    d_qkv = d_qkv.astype(BF).reshape(length, qkv_cols)
    g_qkv = dot(n_0, d_qkv, 0, 0)
    dn_0 = dot(d_qkv, w_qkv_all, 1, 1)

    pre = dot(n_1, w_in_all, 1, 0) + bi
    cdf = 0.5 * (1.0 + lax.erf(pre * 0.7071067811865476))
    act = (pre * cdf).astype(BF)
    slope = cdf + pre * jnp.exp(-0.5 * pre * pre) * 0.3989422804014327
    g_mlp = dot(grad_all, act, 0, 0)
    d_pre = dot(grad_all, w_mlp_t, 1, 0) * slope
    g_bi = jnp.sum(d_pre, axis=0)
    d_pre = d_pre.astype(BF)
    g_in = dot(n_1, d_pre, 0, 0)
    dn_1 = dot(d_pre, w_in_all, 1, 1)
    partial = (dot(flat, w_out_t, 1, 1) + dot(act, w_mlp_t, 1, 1)).astype(BF)

    def reduce(grad):
        grad = grad.astype(BF).reshape(2, n_out, chunk, grad.shape[1])
        got = pair_swap(grad[1], n_dp)
        summed = (grad[0].astype(F32) + got.astype(F32)).astype(BF)
        return jnp.sum(
            outer_exchange(summed, n_dp).reshape(n_out, chunk, -1).astype(F32), axis=0
        )

    r_att = reduce(jnp.concatenate([g_qkv, g_out], axis=1))
    r_mlp = reduce(g_mlp)
    r_in = reduce(g_in)

    def tensor_sum(v):
        v = lax.all_to_all(v, "tensor", 0, 0, tiled=True).reshape(n_t, rows, width)
        return jnp.sum(v.astype(F32), axis=0)

    out = to_own(tokens).astype(F32) + tensor_sum(partial) + adds[0] + adds[1]
    t_sum = tensor_sum((dn_0 * gains[0] + dn_1 * gains[1]).astype(BF))
    own_rows = lax.dynamic_slice_in_dim(xhat, t_index * rows, rows, 0)
    own_rstd = lax.dynamic_slice_in_dim(rstd, t_index * rows, rows, 0)
    d_x = own_rstd * (
        t_sum
        - jnp.mean(t_sum, axis=-1, keepdims=True)
        - own_rows * jnp.mean(t_sum * own_rows, axis=-1, keepdims=True)
    )

    vec = jnp.stack(
        [
            jnp.sum(dn_0 * xhat, axis=0),
            jnp.sum(dn_1 * xhat, axis=0),
            jnp.sum(dn_0, axis=0),
            jnp.sum(dn_1, axis=0),
        ]
    )
    vec = jnp.concatenate([from_own(vec), jnp.sum(cotangent, axis=0)[None]], axis=0)
    vec = vec.reshape(5, n_dp, n_t, piece).transpose(1, 2, 0, 3).reshape(n_dp, n_t, 5 * piece)
    g_bq = g_bq.reshape(heads, n_dp, -1).transpose(1, 0, 2).reshape(n_dp, -1)
    g_bi = g_bi.reshape(b_in.shape[1], n_dp, -1).transpose(1, 0, 2).reshape(n_dp, -1)
    bias = jnp.concatenate([g_bq, g_bi], axis=1)[:, None, :]
    to_me = (jnp.arange(n_t) == t_index)[None, :, None]
    bias = jnp.where(to_me, bias, 0.0)
    vec = jnp.concatenate([vec, bias], axis=2).reshape(n_all, 1, -1)
    vec = jnp.sum(lax.all_to_all(vec, ("dp", "tensor"), 0, 0, tiled=True), axis=(0, 1))
    lead = 5 * piece
    ln = vec[:lead].reshape(5, piece)
    o_bq = vec[lead : lead + n_bq].reshape(b_qkv.shape)
    o_bi = vec[lead + n_bq :].reshape(b_in.shape)

    return (
        from_own(out),
        cotangent + from_own(d_x),
        ln[0:2][None],
        ln[2:4][None],
        jnp.stack([ln[4], ln[4]])[None],
        r_att[:, :qkv_cols].reshape(w_qkv.shape),
        o_bq,
        r_att[:, qkv_cols:].T.reshape(w_out.shape),
        r_in[None],
        o_bi,
        r_mlp.T[None],
    )


def solution(mesh):
    both = ("dp", "tensor")
    in_specs = (
        P(both, None),
        P(both, None),
        P(None, None, both),
        P(None, None, both),
        P(None, None, both),
        P(None, "dp", "tensor", None),
        P(None, "tensor", "dp"),
        P(None, "tensor", None, "dp"),
        P(None, "dp", "tensor"),
        P(None, "tensor", "dp"),
        P(None, "tensor", "dp"),
    )
    out_specs = in_specs[:2] + in_specs[2:]
    return jax.shard_map(local, mesh=mesh, in_specs=in_specs, out_specs=out_specs, check_vma=False)
```

```python
import functools

import jax
import jax.numpy as jnp
from jax import lax
from jax.experimental import pallas as pl
from jax.experimental.pallas import tpu as pltpu
from jax.sharding import PartitionSpec as P


HD = 64
ROT = 16
EPS = 1e-05
BF = jnp.bfloat16
F32 = jnp.float32

LIMIT = 16
BLOCK = 256


def dot(a, b, ca, cb):
    return lax.dot_general(a, b, (((ca,), (cb,)), ((), ())), preferred_element_type=F32)


def call(body, outs, *args, scratch=(), flops=10**9, index=None, limit=LIMIT):
    specs = [pl.BlockSpec(memory_space=pltpu.VMEM)] * len(args)
    if index is not None:
        specs = [pl.BlockSpec(memory_space=pltpu.SMEM)] + specs
        args = (index[None].astype(jnp.int32),) + args
    return pl.pallas_call(
        body,
        out_shape=[jax.ShapeDtypeStruct(s, d) for s, d in outs],
        in_specs=specs,
        out_specs=[pl.BlockSpec(memory_space=pltpu.VMEM)] * len(outs),
        scratch_shapes=list(scratch),
        compiler_params=pltpu.CompilerParams(vmem_limit_bytes=limit * 2**20),
        cost_estimate=pl.CostEstimate(flops=flops, bytes_accessed=4 * 2**20, transcendentals=0),
    )(*args)


def gather_rows(refs, out):
    at = 0
    for r in refs:
        out[at : at + r.shape[0], :] = r[...]
        at += r.shape[0]


def col_sum(v):
    return jnp.sum(v, axis=0, keepdims=True)


def exact_dot(v, hot, ch):
    high = v.astype(BF)
    rest = v - high.astype(F32)
    middle = rest.astype(BF)
    low = (rest - middle.astype(F32)).astype(BF)
    n = v.shape[0]
    got = dot(jnp.concatenate([high, middle, low], axis=0), hot, 1, ch)
    return got[:n] + got[n : 2 * n] + got[2 * n :]


def lanes_of(lane):
    places = lax.broadcasted_iota(jnp.int32, (128, lane.shape[1]), 0)
    return jnp.where(places == lane, 1.0, 0.0).astype(BF)


def prep_kernel(
    tokens, cot, gains, biases, adds, bq, bi, w_qkv, w_out, w_in, w_mlp, source,
    w_att, w_ffn, both, small, cot_sum
):
    heads = w_qkv.shape[0]
    width = tokens.shape[1]
    span = w_qkv.shape[2]
    for h in range(heads):
        w_att[:, h * span : (h + 1) * span] = w_qkv[h]
    w_att[:, heads * span :] = w_out[...].T
    gather_rows((w_in, w_mlp), w_ffn)
    row = lax.broadcasted_iota(jnp.int32, (width, width), 0)
    perm = jnp.where(row == source[0:1, :], 1.0, 0.0).astype(BF)
    one = dot(tokens[...], perm, 1, 0).astype(BF)
    two = dot(cot[...].astype(BF), perm, 1, 0).astype(BF)
    both[:, :width] = one
    both[:, width:] = two
    cot_sum[...] = col_sum(cot[...])
    small[...] = jnp.zeros_like(small)
    full = lambda v: jnp.broadcast_to(v[...].astype(F32)[None], (small.shape[0],) + v.shape)
    piece = gains.shape[1]
    small[:, 0:2, 0:piece] = full(gains)
    small[:, 2:4, 0:piece] = full(biases)
    small[:, 4:5, 0:piece] = full(adds[0:1, :] + adds[1:2, :])
    small[:, 5 : 5 + heads, 0 : bq.shape[1]] = full(bq)
    small[:, 0 : bi.shape[0], 96 : 96 + bi.shape[1]] = full(bi)


def norm_kernel(n_t, index, *refs):
    pieces, refs = refs[:n_t], refs[n_t:]
    small, maps, both, n_0, n_1, xhat_o, vec, bq, bi = refs
    width = n_0.shape[1]
    size = pieces[0].shape[0]
    for k, piece in enumerate(pieces):
        at = jnp.bitwise_xor(index[0], k) * size
        both[pl.ds(pl.multiple_of(at, size), size), :] = piece[...]
    block = min(BLOCK, small.shape[0])
    rows = lax.broadcasted_iota(jnp.int32, (block, width), 0)

    def pick(lane, base, offset, count):
        hot = lanes_of(lane + offset)

        def add_block(b, sums):
            at = pl.multiple_of(b * block, block)
            spread = exact_dot(small[pl.ds(at, block), :], hot, 0)
            return tuple(
                v + col_sum(jnp.where(rows == base - at + r, spread, 0.0))
                for r, v in enumerate(sums)
            )

        zeros = (jnp.zeros((1, width), F32),) * count
        return lax.fori_loop(0, small.shape[0] // block, add_block, zeros)

    lane, base = maps[0:1, :], maps[1:2, :]
    own = pick(lane, base, 0, 4)
    gain, shift = own[:2], own[2:]
    vec[0:1, :] = gain[0]
    vec[1:2, :] = gain[1]
    vec[2:3, :] = pick(maps[2:3, :], maps[3:4, :] + 4, 0, 1)[0]
    bq[...] = pick(maps[4:5, :], maps[5:6, :], 0, 1)[0][:, : bq.shape[1]]
    bi[...] = pick(maps[6:7, :], maps[7:8, :], 96, 1)[0]
    x = both[:, :width].astype(F32)
    centre = x - jnp.mean(x, axis=-1, keepdims=True)
    rstd = lax.rsqrt(jnp.mean(centre * centre, axis=-1, keepdims=True) + EPS)
    xhat = centre * rstd
    xhat_o[...] = xhat
    n_0[...] = (xhat * gain[0] + shift[0]).astype(BF)
    n_1[...] = (xhat * gain[1] + shift[1]).astype(BF)


def pack_kernel(s_0, s_1, cot_sum, g_bq, g_bi, maps, out):
    width = s_0.shape[1]
    block = min(BLOCK, out.shape[0])
    rows = lax.broadcasted_iota(jnp.int32, (block, width), 0)
    g = jnp.concatenate([g_bq[...], jnp.zeros((1, width - g_bq.shape[1]), F32)], axis=1)

    def one_block(b, carry):
        at = pl.multiple_of(b * block, block)

        def put(lane, base, offset, values):
            spread = jnp.zeros(rows.shape, F32)
            for r, v in enumerate(values):
                spread = jnp.where(rows == base - at + r, v, spread)
            return exact_dot(spread, lanes_of(lane + offset), 1)

        lane, base = maps[0:1, :], maps[1:2, :]
        total = put(lane, base, 0, (s_0[0:1, :], s_1[0:1, :], s_0[1:2, :], s_1[1:2, :]))
        total += put(maps[2:3, :], maps[3:4, :] + 4, 0, (cot_sum[...],))
        total += put(maps[4:5, :], maps[5:6, :], 0, (g,))
        total += put(maps[6:7, :], maps[7:8, :], 96, (g_bi[...],))
        out[pl.ds(at, block), :] = total
        return carry

    lax.fori_loop(0, out.shape[0] // block, one_block, 0)


def split_grad(g, own, oth):
    half = own.shape[0]
    own[...] = g[:half].astype(BF)
    oth[...] = g[half:].astype(BF)


def att_kernel(heads, n_chunks, both, n_0, *rest):
    chunks, rest = rest[:n_chunks], rest[n_chunks:]
    bq, tab_c, tab_b, tab_a, w, ctx, dqb, g_own, g_oth, g_bq, qkv, dqkv = rest
    width = n_0.shape[1]
    length = n_0.shape[0]
    cols = heads * 3 * HD
    half = ROT // 2
    gather_rows(chunks, w)
    raw = dot(n_0[...], w[...], 1, 0)[:, : qkv.shape[1]] + bq[...]
    lanes = qkv.shape[1]
    lane = lax.broadcasted_iota(jnp.int32, (1, lanes), 1)
    value_lane = lane >= cols
    for h in range(heads):
        at = (3 * h + 2) * HD
        value_lane = value_lane | ((lane >= at) & (lane < at + HD))
    wide = lambda t, rest: jnp.where(value_lane, rest, jnp.concatenate([t] * (lanes // 128), axis=1))
    t_c, t_b, t_a = wide(tab_c[...], 1.0), wide(tab_b[...], 0.0), wide(tab_a[...], 0.0)
    qkv[...] = (
        raw * t_c + pltpu.roll(raw, lanes - half, 1) * t_b + pltpu.roll(raw, half, 1) * t_a
    ).astype(BF)
    grad = both[:, width:]
    d_ctx = dot(grad, w[...], 1, 0)[:, cols : cols + heads * HD].astype(BF)
    scale = HD ** (-0.5)
    block = length // 2
    dqkv[:, cols:] = jnp.zeros((length, lanes - cols), F32)
    for h in range(heads):
        at = h * 3 * HD
        for i in range(2):
            lo, hi = i * block, (i + 1) * block
            q = qkv[lo:hi, at : at + HD] * jnp.asarray(scale, BF)
            k = qkv[:hi, at + HD : at + 2 * HD]
            v = qkv[:hi, at + 2 * HD : at + 3 * HD]
            s = dot(q, k, 1, 1)
            row = lax.broadcasted_iota(jnp.int32, s.shape, 0) + lo
            col = lax.broadcasted_iota(jnp.int32, s.shape, 1)
            s = jnp.where(col <= row, s, -1e30)
            top = jnp.max(s, axis=-1, keepdims=True)
            e = jnp.exp(s - top)
            p = e * (1.0 / jnp.sum(e, axis=-1, keepdims=True))
            pb = p.astype(BF)
            c = dot(pb, v, 1, 0).astype(BF)
            ctx[lo:hi, h * HD : (h + 1) * HD] = c
            d = d_ctx[lo:hi, h * HD : (h + 1) * HD]
            delta = jnp.sum(d.astype(F32) * c.astype(F32), axis=-1, keepdims=True)
            ds = (p * (dot(d, v, 1, 1) - delta)).astype(BF)
            dqkv[lo:hi, at : at + HD] = dot(ds, k, 1, 0) * scale
            dk, dv = dot(ds, q, 0, 0), dot(pb, d, 0, 0)
            if i == 0:
                dk_0, dv_0 = dk, dv
            else:
                dqkv[:block, at + HD : at + 2 * HD] = dk[:block] + dk_0
                dqkv[block:, at + HD : at + 2 * HD] = dk[block:]
                dqkv[:block, at + 2 * HD : at + 3 * HD] = dv[:block] + dv_0
                dqkv[block:, at + 2 * HD : at + 3 * HD] = dv[block:]
    d = dqkv[...]
    d = d * t_c - pltpu.roll(d, lanes - half, 1) * t_b - pltpu.roll(d, half, 1) * t_a
    g_bq[...] = col_sum(d)
    db = d.astype(BF)
    dqb[...] = db
    g = jnp.concatenate([dot(n_0[...], db, 0, 0)[:, :cols], dot(grad, ctx[...], 0, 0)], axis=1)
    split_grad(g, g_own, g_oth)


def att_tail_kernel(dqb, ctx, w, xhat, vec, t_0, r_0, sums):
    cols = w.shape[1] - ctx.shape[1]
    lanes = dqb.shape[1]
    wide = w[:, :lanes]
    dn = dot(dqb[...], wide, 1, 1)
    sums[0:1, :] = col_sum(dn * xhat[...])
    sums[1:2, :] = col_sum(dn)
    t_0[...] = dn * vec[0:1, :]
    r_0[...] = dot(ctx[...], w[:, cols:], 1, 1)


def ffn_kernel(n_chunks, both, n_1, *rest):
    chunks, rest = rest[:n_chunks], rest[n_chunks:]
    bi, w_in, w_mlp, act, dpb, g_bi, own, *oth = rest
    width = n_1.shape[1]
    size = chunks[0].shape[0] // 2
    for k, c in enumerate(chunks):
        w_in[k * size : (k + 1) * size, :] = c[:size, :]
        w_mlp[k * size : (k + 1) * size, :] = c[size:, :]
    h = dot(n_1[...], w_in[...], 1, 0) + bi[...]
    cdf = 0.5 * (1.0 + lax.erf(h * 0.7071067811865476))
    act[...] = (h * cdf).astype(BF)
    slope = cdf + h * jnp.exp(-0.5 * h * h) * 0.3989422804014327
    grad = both[:, width:]
    d = dot(grad, w_mlp[...], 1, 0) * slope
    g_bi[...] = col_sum(d)
    dpb[...] = d.astype(BF)
    for part, g in enumerate((dot(n_1[...], dpb[...], 0, 0), dot(grad, act[...], 0, 0))):
        g = g.astype(BF)
        rows = slice(part * size, (part + 1) * size)
        for k in range(len(oth)):
            own[k, rows, :] = g[k * size : (k + 1) * size]
            oth[k][rows, :] = g[(len(oth) + k) * size : (len(oth) + k + 1) * size]


def tail_kernel(index, dpb, w_in, act, w_mlp, t_0, r_0, xhat, vec, sums, *rest):
    outs, rt = rest[:-1], rest[-1]
    width = xhat.shape[1]
    dn = dot(dpb[...], w_in[...], 1, 1)
    sums[0:1, :] = col_sum(dn * xhat[...])
    sums[1:2, :] = col_sum(dn)
    rt[:, width:] = (t_0[...] + dn * vec[1:2, :]).astype(BF)
    rt[:, :width] = (r_0[...] + dot(act[...], w_mlp[...], 1, 1)).astype(BF)
    size = outs[0].shape[0]
    for k, out in enumerate(outs):
        at = jnp.bitwise_xor(index[0], k) * size
        out[...] = rt[pl.ds(pl.multiple_of(at, size), size), :]


def add_kernel(own, got, *outs):
    chunk = outs[0].shape[0]
    for k, out in enumerate(outs):
        rows = slice(k * chunk, (k + 1) * chunk)
        out[...] = (own[rows, :].astype(F32) + got[rows, :].astype(F32)).astype(out.dtype)


def add_one_kernel(k, own, *refs):
    *got, out = refs
    out[...] = (own[k].astype(F32) + total_of(got)).astype(out.dtype)


def sum_kernel(*refs):
    *parts, out = refs
    out[...] = total_of(parts).astype(out.dtype)


def total_of(refs):
    total = refs[0][...].astype(F32)
    for r in refs[1:]:
        total = total + r[...].astype(F32)
    return total


def att_out_kernel(*refs):
    *parts, g_qkv, g_out = refs
    total = total_of(parts)
    heads, _, span = g_qkv.shape
    for h in range(heads):
        g_qkv[h] = total[:, h * span : (h + 1) * span]
    g_out[...] = total[:, heads * span :].T


def ffn_out_kernel(*refs):
    *parts, g_in, g_mlp = refs
    total = total_of(parts)
    g_in[...] = total[: g_in.shape[0]]
    g_mlp[...] = total[g_in.shape[0] :]


def small_out_kernel(got, gains, biases, adds, bq, bi):
    total = jnp.sum(got[...], axis=0)
    piece = gains.shape[1]
    first = 5
    gains[...] = total[0:2, 0:piece]
    biases[...] = total[2:4, 0:piece]
    adds[...] = jnp.broadcast_to(total[4:5, 0:piece], adds.shape)
    bq[...] = total[first : first + bq.shape[0], 0 : bq.shape[1]]
    bi[...] = total[0 : bi.shape[0], 96 : 96 + bi.shape[1]]


def rows_kernel(*refs):
    *parts, tokens, cot, vec, source, out, d_in = refs
    width = tokens.shape[1]
    total = total_of(parts)
    row = lax.broadcasted_iota(jnp.int32, (width, width), 0)
    perm = jnp.where(row == source[...], 1.0, 0.0).astype(BF)
    x = tokens[...].astype(F32)
    out[...] = x + exact_dot(total[:, :width], perm, 1) + vec[2:3, :]
    centre = x - jnp.mean(x, axis=-1, keepdims=True)
    rstd = lax.rsqrt(jnp.mean(centre * centre, axis=-1, keepdims=True) + EPS)
    x = centre * rstd
    t = exact_dot(total[:, width:], perm, 1)
    d_in[...] = cot[...] + rstd * (
        t - jnp.mean(t, axis=-1, keepdims=True) - x * jnp.mean(t * x, axis=-1, keepdims=True)
    )


def pair_swap(value, n):
    return lax.ppermute(value, "dp", [(i, i ^ 1) for i in range(n)])


def tensor_swap(value, n, k):
    return lax.ppermute(value, "tensor", [(i, i ^ k) for i in range(n)])


def outer_shift(value, n, k):
    return lax.ppermute(value, "dp", [(i, (i + 2 * k) % n) for i in range(n)])


def rotary_tables(length):
    half = ROT // 2
    inside = jnp.arange(128, dtype=jnp.int32) % HD
    freq = 10000.0 ** (-(inside % half).astype(F32) * 2.0 / ROT)
    angle = jnp.arange(length, dtype=F32)[:, None] * freq[None, :]
    cosine, sine = jnp.cos(angle), jnp.sin(angle)
    return (
        jnp.where(inside < ROT, cosine, 1.0),
        jnp.where(inside < half, -sine, 0.0),
        jnp.where((inside >= half) & (inside < ROT), sine, 0.0),
    )


def local(
    tokens, cotangent, ln_gains, ln_biases, out_biases, w_qkv, b_qkv, w_out, w_in, b_in, w_mlp
):
    n_dp, n_t = lax.axis_size("dp"), lax.axis_size("tensor")
    rows, width = tokens.shape
    length = rows * n_t
    n_out = n_dp // 2
    chunk = width // n_dp
    heads = w_out.shape[1]
    cols = heads * 3 * HD
    lanes = -(-cols // 128) * 128
    hidden = w_in.shape[2]
    inner = lax.axis_index("dp") % 2
    outer = lax.axis_index("dp") // 2
    t_index = lax.axis_index("tensor")
    relay = lambda k: n_out == 4 and k == 2
    near_first = sorted(range(1, n_out), key=lambda k: min(k, n_out - k))

    feature = jnp.arange(width, dtype=jnp.int32)
    half, step, lane = feature // (width // 2), (feature // chunk) % n_out, feature % chunk
    owner = ((outer + step) % n_out) * 2 + jnp.where(half == 1, 1 - inner, inner)
    source = owner * chunk + lane
    n_all = n_dp * n_t
    piece = chunk // n_t
    c_bq, c_bi = b_qkv.shape[2], b_in.shape[2]
    r_bq, r_bi = c_bq * n_dp, c_bi * n_dp
    maps = jnp.stack(
        [
            source % piece,
            source // piece * 8,
            feature % piece,
            feature // piece * 8,
            feature % c_bq,
            jnp.where(
                feature < cols,
                ((feature % r_bq) // c_bq * n_t + t_index) * 8 + 5 + feature // r_bq,
                -8,
            ),
            feature % c_bi,
            ((feature % r_bi) // c_bi * n_t + t_index) * 8 + feature // r_bi,
        ]
    )
    w_att_own, w_ffn_own, both, small, cot_sum = call(
        prep_kernel,
        [((chunk, cols + heads * HD), BF), ((2 * chunk, hidden), BF), ((rows, 2 * width), BF),
         ((n_all, 8, 128), F32), ((1, width), F32)],
        tokens, cotangent, ln_gains[0], ln_biases[0], out_biases[0], b_qkv[0], b_in[0],
        w_qkv[0].transpose(1, 0, 2), w_out[0].reshape(heads * HD, chunk), w_in[0], w_mlp[0].T,
        source[None], limit=56,
    )
    parts = {"att": w_att_own, "ffn": w_ffn_own}

    def fetch(name):
        part = parts[name]
        own, oth = [part] + [None] * (n_out - 1), [None] * n_out
        oth[0] = pair_swap(part, n_dp)
        for k in near_first:
            if relay(k):
                own[n_out - k] = outer_shift(own[n_out - 1], n_dp, 1)
            else:
                own[n_out - k] = outer_shift(part, n_dp, k)
        for k in range(1, n_out):
            oth[k] = pair_swap(own[k], n_dp)
        return own + oth

    c_att = fetch("att")

    small = lax.all_to_all(small, ("dp", "tensor"), 0, 0, tiled=True).reshape(n_all * 8, 128)
    both_parts = [both]
    for k in range(1, n_t):
        low = k & -k
        both_parts.append(tensor_swap(both_parts[k ^ low], n_t, low))
    c_ffn = fetch("ffn")

    seq, big = (length, width), (width, hidden)
    half_att = (width // 2, cols + heads * HD)
    both, n_0, n_1, xhat, vec, bq, bi = call(
        functools.partial(norm_kernel, n_t),
        [((length, 2 * width), BF), (seq, BF), (seq, BF), (seq, F32), ((3, width), F32), ((1, lanes), F32), ((1, hidden), F32)],
        *both_parts, small, maps, index=t_index,
    )
    w_att, ctx, dqb, ga_own, ga_oth, g_bq = call(
        functools.partial(att_kernel, heads, len(c_att)),
        [((width, cols + heads * HD), BF), ((length, heads * HD), BF), ((length, lanes), BF),
         (half_att, BF), (half_att, BF), ((1, lanes), F32)],
        both, n_0, *c_att, bq, *rotary_tables(length),
        scratch=[pltpu.VMEM((length, lanes), BF), pltpu.VMEM((length, lanes), F32)],
    )
    t_0, r_0, s_0 = call(
        att_tail_kernel, [(seq, F32), (seq, F32), ((2, width), F32)],
        dqb, ctx, w_att, xhat, vec,
    )
    w_in_all, w_mlp_t, act, dpb, g_bi, g_own, *g_oth = call(
        functools.partial(ffn_kernel, len(c_ffn)),
        [(big, BF), (big, BF), ((length, hidden), BF), ((length, hidden), BF), ((1, hidden), F32),
         ((n_out, 2 * chunk, hidden), BF)] + [((2 * chunk, hidden), BF)] * n_out,
        both, n_1, *c_ffn, bi,
    )
    s_1, *rt = call(
        tail_kernel, [((2, width), F32)] + [((rows, 2 * width), BF)] * n_t,
        dpb, w_in_all, act, w_mlp_t, t_0, r_0, xhat, vec,
        scratch=[pltpu.VMEM((length, 2 * width), BF)], index=t_index,
    )

    got = pair_swap(ga_oth, n_dp)
    shape = (chunk, cols + heads * HD)
    sums = list(call(add_kernel, [(shape, F32)] + [(shape, BF)] * (n_out - 1), ga_own, got))

    def send(sums, k):
        return outer_shift(sums[k], n_dp, 1 if relay(k) else k)

    for k in [k for k in near_first if relay(k)]:
        (sums[1],) = call(sum_kernel, [(shape, BF)], sums[1], send(sums, k))
        sums[k] = None
    for k in range(1, n_out):
        if sums[k] is not None:
            sums[k] = send(sums, k)
    sums = [v for v in sums if v is not None]
    g_qkv, g_out = call(
        att_out_kernel, [((heads, chunk, 3 * HD), F32), ((heads * HD, chunk), F32)],
        *sums, limit=56,
    )
    sums, relayed = [None] * n_out, []
    for k in sorted(near_first, key=lambda k: (not relay(k), k)) + [0]:
        got = pair_swap(g_oth[k], n_dp)
        (sums[k],) = call(
            functools.partial(add_one_kernel, k),
            [((2 * chunk, hidden), BF if k else F32)], g_own, got, *(relayed if k == 1 else ()),
        )
        if k:
            sums[k] = send(sums, k)
        if relay(k):
            relayed, sums[k] = [sums[k]], None
    sums = [v for v in sums if v is not None]
    g_in, g_mlp = call(ffn_out_kernel, [((chunk, hidden), F32)] * 2, *sums, limit=56)

    for k in range(1, n_t):
        rt[k] = tensor_swap(rt[k], n_t, k)
    out, d_in = call(
        rows_kernel, [((rows, width), F32)] * 2,
        *rt, tokens, cotangent, vec, source[None], limit=56,
    )

    (packed,) = call(
        pack_kernel, [((n_all * 8, 128), F32)],
        s_0, s_1, cot_sum, g_bq, g_bi, maps,
    )
    packed = lax.all_to_all(
        packed.reshape(n_all, 8, 128), ("dp", "tensor"), 0, 0, tiled=True
    )
    small_outs = call(
        small_out_kernel,
        [((2, piece), F32)] * 3 + [((heads, c_bq), F32), ((b_in.shape[1], c_bi), F32)], packed,
    )

    return (
        out,
        d_in,
        small_outs[0][None],
        small_outs[1][None],
        small_outs[2][None],
        g_qkv.transpose(1, 0, 2)[None],
        small_outs[3][None],
        g_out.reshape(w_out.shape),
        g_in[None],
        small_outs[4][None],
        g_mlp.T[None],
    )


def solution(mesh):
    both = ("dp", "tensor")
    in_specs = (
        P(both, None),
        P(both, None),
        P(None, None, both),
        P(None, None, both),
        P(None, None, both),
        P(None, "dp", "tensor", None),
        P(None, "tensor", "dp"),
        P(None, "tensor", None, "dp"),
        P(None, "dp", "tensor"),
        P(None, "tensor", "dp"),
        P(None, "tensor", "dp"),
    )
    return jax.shard_map(local, mesh=mesh, in_specs=in_specs, out_specs=in_specs, check_vma=False)
```

```python
import functools

import jax
import jax.numpy as jnp
from jax import lax
from jax.experimental import pallas as pl
from jax.experimental.pallas import tpu as pltpu
from jax.sharding import PartitionSpec as P


HD = 64
ROT = 16
EPS = 1e-05
BF = jnp.bfloat16
F32 = jnp.float32

LIMIT = 16
BLOCK = 256


def dot(a, b, ca, cb):
    return lax.dot_general(a, b, (((ca,), (cb,)), ((), ())), preferred_element_type=F32)


def call(body, outs, *args, scratch=(), flops=10**9, index=None, limit=LIMIT):
    specs = [pl.BlockSpec(memory_space=pltpu.VMEM)] * len(args)
    if index is not None:
        specs = [pl.BlockSpec(memory_space=pltpu.SMEM)] + specs
        args = (index[None].astype(jnp.int32),) + args
    return pl.pallas_call(
        body,
        out_shape=[jax.ShapeDtypeStruct(s, d) for s, d in outs],
        in_specs=specs,
        out_specs=[pl.BlockSpec(memory_space=pltpu.VMEM)] * len(outs),
        scratch_shapes=list(scratch),
        compiler_params=pltpu.CompilerParams(vmem_limit_bytes=limit * 2**20),
        cost_estimate=pl.CostEstimate(flops=flops, bytes_accessed=4 * 2**20, transcendentals=0),
    )(*args)


def gather_rows(refs, out):
    at = 0
    for r in refs:
        out[at : at + r.shape[0], :] = r[...]
        at += r.shape[0]


def col_sum(v):
    return jnp.sum(v, axis=0, keepdims=True)


def exact_dot(v, hot, ch):
    high = v.astype(BF)
    rest = v - high.astype(F32)
    middle = rest.astype(BF)
    low = (rest - middle.astype(F32)).astype(BF)
    n = v.shape[0]
    got = dot(jnp.concatenate([high, middle, low], axis=0), hot, 1, ch)
    return got[:n] + got[n : 2 * n] + got[2 * n :]


def lanes_of(lane):
    places = lax.broadcasted_iota(jnp.int32, (128, lane.shape[1]), 0)
    return jnp.where(places == lane, 1.0, 0.0).astype(BF)


def weights_kernel(w_qkv, w_out, w_in, w_mlp, w_att, w_ffn):
    heads, _, span = w_qkv.shape
    for h in range(heads):
        w_att[:, h * span : (h + 1) * span] = w_qkv[h]
    w_att[:, heads * span :] = w_out[...].T
    gather_rows((w_in, w_mlp), w_ffn)


def prep_kernel(
    heads, tokens, cot, gains, biases, adds, bq, bi, source, both, small, cot_sum
):
    width = tokens.shape[1]
    row = lax.broadcasted_iota(jnp.int32, (width, width), 0)
    perm = jnp.where(row == source[0:1, :], 1.0, 0.0).astype(BF)
    one = dot(tokens[...], perm, 1, 0).astype(BF)
    two = dot(cot[...].astype(BF), perm, 1, 0).astype(BF)
    both[:, :width] = one
    both[:, width:] = two
    cot_sum[...] = col_sum(cot[...])
    small[...] = jnp.zeros_like(small)
    full = lambda v: jnp.broadcast_to(v[...].astype(F32)[None], (small.shape[0],) + v.shape)
    piece = gains.shape[1]
    small[:, 0:2, 0:piece] = full(gains)
    small[:, 2:4, 0:piece] = full(biases)
    small[:, 4:5, 0:piece] = full(adds[0:1, :] + adds[1:2, :])
    small[:, 5 : 5 + heads, 0 : bq.shape[1]] = full(bq)
    small[:, 0 : bi.shape[0], 96 : 96 + bi.shape[1]] = full(bi)


def norm_kernel(n_t, index, *refs):
    pieces, refs = refs[:n_t], refs[n_t:]
    small, maps, _, _, _, both, n_0, n_1, xhat_o, vec, bq, bi = refs
    width = n_0.shape[1]
    size = pieces[0].shape[0]
    for k, piece in enumerate(pieces):
        at = jnp.bitwise_xor(index[0], k) * size
        both[pl.ds(pl.multiple_of(at, size), size), :] = piece[...]
    block = min(BLOCK, small.shape[0])
    rows = lax.broadcasted_iota(jnp.int32, (block, width), 0)

    def pick(lane, base, offset, count):
        hot = lanes_of(lane + offset)

        def add_block(b, sums):
            at = pl.multiple_of(b * block, block)
            spread = exact_dot(small[pl.ds(at, block), :], hot, 0)
            return tuple(
                v + col_sum(jnp.where(rows == base - at + r, spread, 0.0))
                for r, v in enumerate(sums)
            )

        zeros = (jnp.zeros((1, width), F32),) * count
        return lax.fori_loop(0, small.shape[0] // block, add_block, zeros)

    lane, base = maps[0:1, :], maps[1:2, :]
    own = pick(lane, base, 0, 4)
    gain, shift = own[:2], own[2:]
    vec[0:1, :] = gain[0]
    vec[1:2, :] = gain[1]
    vec[2:3, :] = pick(maps[2:3, :], maps[3:4, :] + 4, 0, 1)[0]
    bq[...] = pick(maps[4:5, :], maps[5:6, :], 0, 1)[0][:, : bq.shape[1]]
    bi[...] = pick(maps[6:7, :], maps[7:8, :], 96, 1)[0]
    x = both[:, :width].astype(F32)
    centre = x - jnp.mean(x, axis=-1, keepdims=True)
    rstd = lax.rsqrt(jnp.mean(centre * centre, axis=-1, keepdims=True) + EPS)
    xhat = centre * rstd
    xhat_o[...] = xhat
    n_0[...] = (xhat * gain[0] + shift[0]).astype(BF)
    n_1[...] = (xhat * gain[1] + shift[1]).astype(BF)


def pack_kernel(s_0, s_1, cot_sum, g_bq, g_bi, maps, out):
    width = s_0.shape[1]
    block = min(BLOCK, out.shape[0])
    rows = lax.broadcasted_iota(jnp.int32, (block, width), 0)
    g = jnp.concatenate([g_bq[...], jnp.zeros((1, width - g_bq.shape[1]), F32)], axis=1)

    def one_block(b, carry):
        at = pl.multiple_of(b * block, block)

        def put(lane, base, offset, values):
            spread = jnp.zeros(rows.shape, F32)
            for r, v in enumerate(values):
                spread = jnp.where(rows == base - at + r, v, spread)
            return exact_dot(spread, lanes_of(lane + offset), 1)

        lane, base = maps[0:1, :], maps[1:2, :]
        total = put(lane, base, 0, (s_0[0:1, :], s_1[0:1, :], s_0[1:2, :], s_1[1:2, :]))
        total += put(maps[2:3, :], maps[3:4, :] + 4, 0, (cot_sum[...],))
        total += put(maps[4:5, :], maps[5:6, :], 0, (g,))
        total += put(maps[6:7, :], maps[7:8, :], 96, (g_bi[...],))
        out[pl.ds(at, block), :] = total
        return carry

    lax.fori_loop(0, out.shape[0] // block, one_block, 0)


def split_grad(g, at, own, far, near):
    n = own.shape[0]
    size = g.shape[0] // (2 * n)
    for k in range(n):
        own[k, at : at + size, :] = g[k * size : (k + 1) * size]
        out, slot = (near, k) if k < near.shape[0] else (far, k - near.shape[0])
        out[slot, at : at + size, :] = g[(n + k) * size : (n + k + 1) * size]


def att_kernel(heads, n_chunks, both, n_0, *rest):
    chunks, rest = rest[:n_chunks], rest[n_chunks:]
    bq, tab_c, tab_b, tab_a, w, ctx, dqb, g_bq, g_own, g_far, g_near, qkv, dqkv = rest
    width = n_0.shape[1]
    length = n_0.shape[0]
    cols = heads * 3 * HD
    half = ROT // 2
    gather_rows(chunks, w)
    raw = dot(n_0[...], w[...], 1, 0)[:, : qkv.shape[1]] + bq[...]
    lanes = qkv.shape[1]
    lane = lax.broadcasted_iota(jnp.int32, (1, lanes), 1)
    value_lane = lane >= cols
    for h in range(heads):
        at = (3 * h + 2) * HD
        value_lane = value_lane | ((lane >= at) & (lane < at + HD))
    wide = lambda t, rest: jnp.where(value_lane, rest, jnp.concatenate([t] * (lanes // 128), axis=1))
    t_c, t_b, t_a = wide(tab_c[...], 1.0), wide(tab_b[...], 0.0), wide(tab_a[...], 0.0)
    qkv[...] = (
        raw * t_c + pltpu.roll(raw, lanes - half, 1) * t_b + pltpu.roll(raw, half, 1) * t_a
    ).astype(BF)
    grad = both[:, width:]
    d_ctx = dot(grad, w[...], 1, 0)[:, cols : cols + heads * HD].astype(BF)
    scale = HD ** (-0.5)
    block = length // 2
    dqkv[:, cols:] = jnp.zeros((length, lanes - cols), F32)
    for h in range(heads):
        at = h * 3 * HD
        for i in range(2):
            lo, hi = i * block, (i + 1) * block
            q = qkv[lo:hi, at : at + HD] * jnp.asarray(scale, BF)
            k = qkv[:hi, at + HD : at + 2 * HD]
            v = qkv[:hi, at + 2 * HD : at + 3 * HD]
            s = dot(q, k, 1, 1)
            row = lax.broadcasted_iota(jnp.int32, s.shape, 0) + lo
            col = lax.broadcasted_iota(jnp.int32, s.shape, 1)
            s = jnp.where(col <= row, s, -1e30)
            top = jnp.max(s, axis=-1, keepdims=True)
            e = jnp.exp(s - top)
            p = e * (1.0 / jnp.sum(e, axis=-1, keepdims=True))
            pb = p.astype(BF)
            c = dot(pb, v, 1, 0).astype(BF)
            ctx[lo:hi, h * HD : (h + 1) * HD] = c
            d = d_ctx[lo:hi, h * HD : (h + 1) * HD]
            delta = jnp.sum(d.astype(F32) * c.astype(F32), axis=-1, keepdims=True)
            ds = (p * (dot(d, v, 1, 1) - delta)).astype(BF)
            dqkv[lo:hi, at : at + HD] = dot(ds, k, 1, 0) * scale
            dk, dv = dot(ds, q, 0, 0), dot(pb, d, 0, 0)
            if i == 0:
                dk_0, dv_0 = dk, dv
            else:
                dqkv[:block, at + HD : at + 2 * HD] = dk[:block] + dk_0
                dqkv[block:, at + HD : at + 2 * HD] = dk[block:]
                dqkv[:block, at + 2 * HD : at + 3 * HD] = dv[:block] + dv_0
                dqkv[block:, at + 2 * HD : at + 3 * HD] = dv[block:]
    d = dqkv[...]
    d = d * t_c - pltpu.roll(d, lanes - half, 1) * t_b - pltpu.roll(d, half, 1) * t_a
    g_bq[...] = col_sum(d)
    db = d.astype(BF)
    dqb[...] = db
    g = jnp.concatenate([dot(n_0[...], db, 0, 0)[:, :cols], dot(grad, ctx[...], 0, 0)], axis=1)
    split_grad(g.astype(BF), 0, g_own, g_far, g_near)


def att_tail_kernel(dqb, ctx, w, xhat, vec, t_0, r_0, sums):
    cols = w.shape[1] - ctx.shape[1]
    lanes = dqb.shape[1]
    wide = w[:, :lanes]
    dn = dot(dqb[...], wide, 1, 1)
    sums[0:1, :] = col_sum(dn * xhat[...])
    sums[1:2, :] = col_sum(dn)
    t_0[...] = dn * vec[0:1, :]
    r_0[...] = dot(ctx[...], w[:, cols:], 1, 1)


def ffn_kernel(n_chunks, both, n_1, *rest):
    chunks, rest = rest[:n_chunks], rest[n_chunks:]
    bi, w_in, w_mlp, act, dpb, g_bi, own, far, near = rest
    width = n_1.shape[1]
    size = chunks[0].shape[0] // 2
    for k, c in enumerate(chunks):
        w_in[k * size : (k + 1) * size, :] = c[:size, :]
        w_mlp[k * size : (k + 1) * size, :] = c[size:, :]
    h = dot(n_1[...], w_in[...], 1, 0) + bi[...]
    cdf = 0.5 * (1.0 + lax.erf(h * 0.7071067811865476))
    act[...] = (h * cdf).astype(BF)
    slope = cdf + h * jnp.exp(-0.5 * h * h) * 0.3989422804014327
    grad = both[:, width:]
    d = dot(grad, w_mlp[...], 1, 0) * slope
    g_bi[...] = col_sum(d)
    dpb[...] = d.astype(BF)
    for part, g in enumerate((dot(n_1[...], dpb[...], 0, 0), dot(grad, act[...], 0, 0))):
        split_grad(g.astype(BF), part * size, own, far, near)


def tail_kernel(index, dpb, w_in, act, w_mlp, t_0, r_0, xhat, vec, sums, *rest):
    outs, rt = rest[:-1], rest[-1]
    width = xhat.shape[1]
    dn = dot(dpb[...], w_in[...], 1, 1)
    sums[0:1, :] = col_sum(dn * xhat[...])
    sums[1:2, :] = col_sum(dn)
    rt[:, width:] = (t_0[...] + dn * vec[1:2, :]).astype(BF)
    rt[:, :width] = (r_0[...] + dot(act[...], w_mlp[...], 1, 1)).astype(BF)
    size = outs[0].shape[0]
    for k, out in enumerate(outs):
        at = jnp.bitwise_xor(index[0], k) * size
        out[...] = rt[pl.ds(pl.multiple_of(at, size), size), :]


def add_kernel(first, own, got, *outs):
    for k, out in enumerate(outs):
        out[...] = (own[first + k].astype(F32) + got[k].astype(F32)).astype(out.dtype)


def add_more_kernel(own, got, *refs):
    *more, out = refs
    total = own[1].astype(F32) + got[1].astype(F32)
    for r in more:
        total = total + r[...].astype(F32)
    out[...] = total.astype(out.dtype)


def total_of(refs):
    total = refs[0][...].astype(F32)
    for r in refs[1:]:
        total = total + r[...].astype(F32)
    return total


def own_total(own, got, *refs):
    total = own[0].astype(F32) + got[0].astype(F32)
    return total + total_of(refs)


def att_out_kernel(*refs):
    *parts, g_qkv, g_out = refs
    total = own_total(*parts)
    heads, _, span = g_qkv.shape
    for h in range(heads):
        g_qkv[h] = total[:, h * span : (h + 1) * span]
    g_out[...] = total[:, heads * span :].T


def ffn_out_kernel(*refs):
    *parts, g_in, g_mlp = refs
    total = own_total(*parts)
    g_in[...] = total[: g_in.shape[0]]
    g_mlp[...] = total[g_in.shape[0] :]


def small_out_kernel(got, gains, biases, adds, bq, bi):
    total = jnp.sum(got[...], axis=0)
    piece = gains.shape[1]
    first = 5
    gains[...] = total[0:2, 0:piece]
    biases[...] = total[2:4, 0:piece]
    adds[...] = jnp.broadcast_to(total[4:5, 0:piece], adds.shape)
    bq[...] = total[first : first + bq.shape[0], 0 : bq.shape[1]]
    bi[...] = total[0 : bi.shape[0], 96 : 96 + bi.shape[1]]


def rows_kernel(*refs):
    *parts, tokens, cot, vec, source, out, d_in = refs
    width = tokens.shape[1]
    total = total_of(parts)
    row = lax.broadcasted_iota(jnp.int32, (width, width), 0)
    perm = jnp.where(row == source[...], 1.0, 0.0).astype(BF)
    x = tokens[...].astype(F32)
    size = tokens.shape[0]
    both = exact_dot(jnp.concatenate([total[:, :width], total[:, width:]], axis=0), perm, 1)
    out[...] = x + both[:size] + vec[2:3, :]
    centre = x - jnp.mean(x, axis=-1, keepdims=True)
    rstd = lax.rsqrt(jnp.mean(centre * centre, axis=-1, keepdims=True) + EPS)
    x = centre * rstd
    t = both[size:]
    d_in[...] = cot[...] + rstd * (
        t - jnp.mean(t, axis=-1, keepdims=True) - x * jnp.mean(t * x, axis=-1, keepdims=True)
    )


def pair_swap(value, n):
    return lax.ppermute(value, "dp", [(i, i ^ 1) for i in range(n)])


def tensor_swap(value, n, k):
    return lax.ppermute(value, "tensor", [(i, i ^ k) for i in range(n)])


def outer_shift(value, n, k):
    return lax.ppermute(value, "dp", [(i, (i + 2 * k) % n) for i in range(n)])


def rotary_tables(length):
    half = ROT // 2
    inside = jnp.arange(128, dtype=jnp.int32) % HD
    freq = 10000.0 ** (-(inside % half).astype(F32) * 2.0 / ROT)
    angle = jnp.arange(length, dtype=F32)[:, None] * freq[None, :]
    cosine, sine = jnp.cos(angle), jnp.sin(angle)
    return (
        jnp.where(inside < ROT, cosine, 1.0),
        jnp.where(inside < half, -sine, 0.0),
        jnp.where((inside >= half) & (inside < ROT), sine, 0.0),
    )


def local(
    tokens, cotangent, ln_gains, ln_biases, out_biases, w_qkv, b_qkv, w_out, w_in, b_in, w_mlp
):
    n_dp, n_t = lax.axis_size("dp"), lax.axis_size("tensor")
    rows, width = tokens.shape
    length = rows * n_t
    n_out = n_dp // 2
    chunk = width // n_dp
    heads = w_out.shape[1]
    cols = heads * 3 * HD
    lanes = -(-cols // 128) * 128
    hidden = w_in.shape[2]
    inner = lax.axis_index("dp") % 2
    outer = lax.axis_index("dp") // 2
    t_index = lax.axis_index("tensor")
    relay = lambda k: n_out == 4 and k == 2
    near_first = sorted(range(1, n_out), key=lambda k: min(k, n_out - k))

    feature = jnp.arange(width, dtype=jnp.int32)
    half, step, lane = feature // (width // 2), (feature // chunk) % n_out, feature % chunk
    owner = ((outer + step) % n_out) * 2 + jnp.where(half == 1, 1 - inner, inner)
    source = owner * chunk + lane
    n_all = n_dp * n_t
    piece = chunk // n_t
    c_bq, c_bi = b_qkv.shape[2], b_in.shape[2]
    r_bq, r_bi = c_bq * n_dp, c_bi * n_dp
    maps = jnp.stack(
        [
            source % piece,
            source // piece * 8,
            feature % piece,
            feature // piece * 8,
            feature % c_bq,
            jnp.where(
                feature < cols,
                ((feature % r_bq) // c_bq * n_t + t_index) * 8 + 5 + feature // r_bq,
                -8,
            ),
            feature % c_bi,
            ((feature % r_bi) // c_bi * n_t + t_index) * 8 + feature // r_bi,
        ]
    )
    w_att_own, w_ffn_own = call(
        weights_kernel,
        [((chunk, cols + heads * HD), BF), ((2 * chunk, hidden), BF)],
        w_qkv[0].transpose(1, 0, 2), w_out[0].reshape(heads * HD, chunk), w_in[0], w_mlp[0].T,
        limit=56,
    )
    both, small, cot_sum = call(
        functools.partial(prep_kernel, heads),
        [((rows, 2 * width), BF), ((n_all, 8, 128), F32), ((1, width), F32)],
        tokens, cotangent, ln_gains[0], ln_biases[0], out_biases[0], b_qkv[0], b_in[0],
        source[None], limit=56,
    )
    parts = {"att": w_att_own, "ffn": w_ffn_own}

    def fetch(name):
        part = parts[name]
        own, oth = [part] + [None] * (n_out - 1), [None] * n_out
        oth[0] = pair_swap(part, n_dp)
        for k in near_first:
            if relay(k):
                own[n_out - k] = outer_shift(own[n_out - 1], n_dp, 1)
            else:
                own[n_out - k] = outer_shift(part, n_dp, k)
        for k in range(1, n_out):
            oth[k] = pair_swap(own[k], n_dp)
        return own + oth

    c_att = fetch("att")

    small = lax.all_to_all(small, ("dp", "tensor"), 0, 0, tiled=True).reshape(n_all * 8, 128)
    both_parts = [both]
    for k in range(1, n_t):
        low = k & -k
        both_parts.append(tensor_swap(both_parts[k ^ low], n_t, low))
    c_ffn = fetch("ffn")

    seq, big = (length, width), (width, hidden)
    tables = rotary_tables(length)
    both, n_0, n_1, xhat, vec, bq, bi = call(
        functools.partial(norm_kernel, n_t),
        [((length, 2 * width), BF), (seq, BF), (seq, BF), (seq, F32), ((3, width), F32), ((1, lanes), F32), ((1, hidden), F32)],
        *both_parts, small, maps, *tables, index=t_index,
    )
    w_att, ctx, dqb, g_bq, *g_att = call(
        functools.partial(att_kernel, heads, len(c_att)),
        [((width, cols + heads * HD), BF), ((length, heads * HD), BF), ((length, lanes), BF),
         ((1, lanes), F32), ((n_out, chunk, cols + heads * HD), BF),
         ((n_out - 2, chunk, cols + heads * HD), BF), ((2, chunk, cols + heads * HD), BF)],
        both, n_0, *c_att, bq, *tables,
        scratch=[pltpu.VMEM((length, lanes), BF), pltpu.VMEM((length, lanes), F32)],
    )
    t_0, r_0, s_0 = call(
        att_tail_kernel, [(seq, F32), (seq, F32), ((2, width), F32)],
        dqb, ctx, w_att, xhat, vec,
    )
    w_in_all, w_mlp_t, act, dpb, g_bi, *g_ffn = call(
        functools.partial(ffn_kernel, len(c_ffn)),
        [(big, BF), (big, BF), ((length, hidden), BF), ((length, hidden), BF), ((1, hidden), F32),
         ((n_out, 2 * chunk, hidden), BF), ((n_out - 2, 2 * chunk, hidden), BF),
         ((2, 2 * chunk, hidden), BF)],
        both, n_1, *c_ffn, bi,
    )
    s_1, *rt = call(
        tail_kernel, [((2, width), F32)] + [((rows, 2 * width), BF)] * n_t,
        dpb, w_in_all, act, w_mlp_t, t_0, r_0, xhat, vec,
        scratch=[pltpu.VMEM((length, 2 * width), BF)], index=t_index,
    )

    def reduce(own, far, near):
        shape = own.shape[1:]

        def onward(v, places):
            return outer_shift(v, n_dp, places)

        far = pair_swap(far, n_dp)
        near = pair_swap(near, n_dp)
        sums = call(
            functools.partial(add_kernel, 2), [(shape, BF)] * (n_out - 2),
            own, far,
        )
        more, last = [], []
        for k, v in zip(range(2, n_out), sums):
            (more if relay(k) else last).append(onward(v, 1 if relay(k) else k))
        (one,) = call(add_more_kernel, [(shape, BF)], own, near, *more)
        return [own, near, *last, onward(one, 1)]

    g_qkv, g_out = call(
        att_out_kernel, [((heads, chunk, 3 * HD), F32), ((heads * HD, chunk), F32)],
        *reduce(*g_att),
    )
    g_in, g_mlp = call(ffn_out_kernel, [((chunk, hidden), F32)] * 2, *reduce(*g_ffn))

    for k in range(1, n_t):
        rt[k] = tensor_swap(rt[k], n_t, k)
    out, d_in = call(
        rows_kernel, [((rows, width), F32)] * 2,
        *rt, tokens, cotangent, vec, source[None], limit=56,
    )

    (packed,) = call(
        pack_kernel, [((n_all * 8, 128), F32)],
        s_0, s_1, cot_sum, g_bq, g_bi, maps,
    )
    packed = lax.all_to_all(
        packed.reshape(n_all, 8, 128), ("dp", "tensor"), 0, 0, tiled=True
    )
    small_outs = call(
        small_out_kernel,
        [((2, piece), F32)] * 3 + [((heads, c_bq), F32), ((b_in.shape[1], c_bi), F32)], packed,
    )

    return (
        out,
        d_in,
        small_outs[0][None],
        small_outs[1][None],
        small_outs[2][None],
        g_qkv.transpose(1, 0, 2)[None],
        small_outs[3][None],
        g_out.reshape(w_out.shape),
        g_in[None],
        small_outs[4][None],
        g_mlp.T[None],
    )


def solution(mesh):
    both = ("dp", "tensor")
    in_specs = (
        P(both, None),
        P(both, None),
        P(None, None, both),
        P(None, None, both),
        P(None, None, both),
        P(None, "dp", "tensor", None),
        P(None, "tensor", "dp"),
        P(None, "tensor", None, "dp"),
        P(None, "dp", "tensor"),
        P(None, "tensor", "dp"),
        P(None, "tensor", "dp"),
    )
    return jax.shard_map(local, mesh=mesh, in_specs=in_specs, out_specs=in_specs, check_vma=False)
```
